32 devices in a mesh: ctx: 16 (over z, y, core), tp: 2 (over x).
Axes of the slice: x: 2, y: 2, z: 4, core: 2. Of those that a mesh axis runs over, the one named last changes fastest.
Arguments:
- key_value: bfloat16 [4096, 4, 256], P('ctx', 'tp'), may hold values from -6 to 6
- queries: bfloat16 [4096, 32, 128], P('ctx', 'tp')
- doc_lengths: int32 [8], replicated, may hold values from 1 to 1024, 4096 in all
Outputs:
- attended: bfloat16 [4096, 32, 128], P('ctx', 'tp')
The draws below stay inside these ranges and needn't reach their ends.
Inputs may be any that keep to these rules, and one draw needn't show every extreme that they name: `doc_lengths`: the lengths sum to 4096 and the longest is exactly 1024.
All inputs are finite; a program needn't handle non-finite values.
Results may differ from the reference program's by a relative error of at most 0.017.
The reference program's roundings to bfloat16 on the way (of `rotated_kv`, `rotated` and `rounded_weights`) count: a program that leaves them out, or rounds other values in their place, can miss the bound.
Values may be sent and summed in bfloat16 or wider, within the bound.
No kernel may reach another device: no remote copies, remote signals or barrier semaphores. Data moves between devices by JAX's collectives and lax.ppermute only.
A program may use at most 64 MiB of HBM per device.

```python
import math
import jax
import jax.numpy as jnp
import numpy as np
from jax import lax

QHEADS = 32
KVHEADS = 4
HEAD = 128
BLOCK = 256
GROUP = 8
SEQ = 4096
MAXDOC = 1024
NDOCS = 8
N_CTX = 16


def draw_queries(key, part):
    base = jnp.clip(jax.random.normal(key, (SEQ, QHEADS, HEAD), jnp.float32), -6.0, 6.0)
    return base.astype(jnp.bfloat16)


def block_scale(rng, dims, pieces, low, top_value):
    factor_of = 1.0
    for axis_at, blocks in pieces:
        draws = jax.random.uniform(jax.random.fold_in(jax.random.fold_in(rng, 6), axis_at), (blocks,), jnp.float32, low / len(pieces), top_value / len(pieces))
        factor_of = factor_of * jnp.repeat(jnp.exp(draws), dims[axis_at] // blocks).reshape((-1,) + (1,) * (len(dims) - 1 - axis_at))
    return factor_of


def length_profile(count, total, bound, lean):
    portions = [(1 << 20) // math.isqrt(standing ** lean) + 1 for standing in range(2, count + 1)]
    spare, counts = total - bound - (count - 1), [1] * (count - 1)
    while spare > 0:
        free = [i for i in range(count - 1) if counts[i] < bound]
        mass, left = sum([portions[i] for i in free]), spare
        for i in free:
            extra = min(bound - counts[i], max(1, left * portions[i] // mass), spare)
            counts[i] = counts[i] + extra
            spare = spare - extra
    return np.array([bound] + counts)


def ragged(key, amount, total, reach, slope):
    if amount == 2:
        one = jax.random.randint(key, (), max(1, total - reach), min(reach, total - 1) + 1)
        return jnp.stack([one, total - one])
    sizes = jnp.asarray(length_profile(amount, total, reach, slope), jnp.int32)
    couples = (amount - 1) // 2
    donor, receiver = sizes[1:1 + 2 * couples:2], sizes[2:2 + 2 * couples:2]
    margin = jnp.minimum(donor - 1, reach - receiver)
    moved = jax.random.randint(jax.random.fold_in(key, 1), (couples,), 0, 1 << 20) % (margin + 1)
    sizes = sizes.at[1:1 + 2 * couples:2].set(donor - moved).at[2:2 + 2 * couples:2].set(receiver + moved)
    return sizes[jax.random.permutation(jax.random.fold_in(key, 2), amount)]


def noise(stream_key, dims, scale, limit, split=(), kind=jnp.bfloat16):
    entries = jax.random.normal(stream_key, dims, jnp.float32) * scale
    if len(split) > 0:
        entries = block_scale(stream_key, dims, split, -0.22, 0.18) * entries
    return jnp.clip(entries, min=-limit, max=limit).astype(kind)


def setup_inputs(seed: int = 0) -> dict:
    arg_keys = jax.random.split(jax.random.key(seed), 4)
    return {
        "key_value": noise(arg_keys[0], (SEQ, KVHEADS, 2 * HEAD), 1.0, 6.0, ((0, 16), (1, 2))),
        "queries": draw_queries(jax.random.fold_in(arg_keys[3], 71), 0),
        "doc_lengths": ragged(arg_keys[2], NDOCS, SEQ, MAXDOC, 2).astype(jnp.int32),
    }


ROPE_BASE = 500000.0
MASKED = -1.0e30


def rotate(vectors, positions):
    width = vectors.shape[-1]
    half = width // 2
    inverse_freq = ROPE_BASE ** (-(jnp.arange(half, dtype=jnp.float32) * 2.0 / width))
    angles = positions.astype(jnp.float32)[..., None] * inverse_freq
    cosine = jnp.cos(angles)[..., None, :]
    sine_part = jnp.sin(angles)[..., None, :]
    front_half = vectors[..., :half]
    back_half = vectors[..., half:]
    return jnp.concatenate([front_half * cosine - back_half * sine_part, back_half * cosine + front_half * sine_part], axis=-1)


def reference(key_value, queries, doc_lengths):
    half = BLOCK // 2
    last_block = 2 * N_CTX - 1
    row_ids = jnp.arange(SEQ, dtype=jnp.int32)
    device = row_ids // BLOCK
    local = row_ids % BLOCK
    block = jnp.where(local < half, device, last_block - device).astype(jnp.int32)
    positions = (block * half + local % half).astype(jnp.int32)
    pos_ids = jnp.arange(SEQ, dtype=jnp.int32)
    pos_block = pos_ids // half
    pos_device = jnp.where(pos_block < N_CTX, pos_block, last_block - pos_block).astype(jnp.int32)
    pos_upper = (pos_block >= N_CTX).astype(jnp.int32)
    row_of_position = (pos_device * BLOCK + pos_upper * half + pos_ids % half).astype(jnp.int32)
    doc_ends = jnp.cumsum(doc_lengths).astype(jnp.int32)
    document = jnp.sum((pos_ids[:, None] >= doc_ends[None, :]).astype(jnp.int32), axis=1).astype(jnp.int32)
    kv_sorted = jnp.take(key_value, row_of_position, axis=0)
    q_sorted = jnp.take(queries, row_of_position, axis=0)
    rotated_kv = jnp.concatenate([rotate(kv_sorted[..., :HEAD].astype(jnp.float32), pos_ids), kv_sorted[..., HEAD:].astype(jnp.float32)], axis=-1).astype(jnp.bfloat16)
    rotated = rotate(q_sorted.astype(jnp.float32), pos_ids).astype(jnp.bfloat16).reshape(SEQ, KVHEADS, GROUP, HEAD)
    padded_kv = jnp.concatenate([jnp.zeros((MAXDOC, KVHEADS, 2 * HEAD), jnp.bfloat16), rotated_kv], axis=0)
    padded_pos = jnp.concatenate([jnp.full((MAXDOC,), -1, jnp.int32), pos_ids], axis=0)
    padded_doc = jnp.concatenate([jnp.full((MAXDOC,), -1, jnp.int32), document], axis=0)
    score_scale = 1.0 / (HEAD ** 0.5)
    block_rows = min(512, SEQ)
    block_count = SEQ // block_rows
    span = MAXDOC + block_rows

    def per_head(index):
        key_all = padded_kv[:, index]

        def per_block(number):
            start = (number * block_rows).astype(jnp.int32)
            keys = lax.dynamic_slice_in_dim(key_all, start, span, 0).astype(jnp.float32)
            key_pos = lax.dynamic_slice_in_dim(padded_pos, start, span, 0)
            key_doc = lax.dynamic_slice_in_dim(padded_doc, start, span, 0)
            query_block = lax.dynamic_slice_in_dim(rotated[:, index], start, block_rows, 0).astype(jnp.float32)
            query_pos = lax.dynamic_slice_in_dim(pos_ids, start, block_rows, 0)
            query_doc = lax.dynamic_slice_in_dim(document, start, block_rows, 0)
            scores = jnp.einsum("bgc,nc->bgn", query_block, keys[:, :HEAD], precision=lax.Precision.HIGHEST) * score_scale
            allowed = (key_doc[None, :] == query_doc[:, None]) & (key_pos[None, :] <= query_pos[:, None])
            visible = allowed[:, None, :]
            largest = jnp.max(jnp.where(visible, scores, MASKED), axis=-1)
            weights = jnp.where(visible, jnp.exp(scores - largest[..., None]), 0.0)
            total = jnp.sum(weights, axis=-1)
            rounded_weights = lax.optimization_barrier(weights.astype(jnp.bfloat16)).astype(jnp.float32)
            summed = jnp.einsum("bgn,nc->bgc", rounded_weights, keys[:, HEAD:], precision=lax.Precision.HIGHEST)
            return summed / total[..., None]

        outputs = lax.map(per_block, jnp.arange(block_count, dtype=jnp.int32))
        return outputs.reshape(SEQ, GROUP, HEAD)

    result = lax.map(per_head, jnp.arange(KVHEADS, dtype=jnp.int32))
    in_order = jnp.transpose(result, (1, 0, 2, 3)).reshape(SEQ, QHEADS, HEAD)
    return jnp.take(in_order, positions, axis=0).astype(jnp.bfloat16)
```

```python
import functools
import math

import jax
import jax.numpy as jnp
import numpy as np
from jax import lax
from jax.experimental import pallas as pl
from jax.experimental.pallas import tpu as pltpu
from jax.sharding import PartitionSpec as P

ROPE_BASE = 500000.0
HIDDEN = -3.0e38
REACH = 4


def chain_device(chunk, chips):
    return 2 * chunk if chunk < chips else 2 * (2 * chips - 1 - chunk) + 1


def along_chain(value, steps):
    count = lax.axis_size("ctx")
    chips = count // 2
    pairs = [
        (chain_device(c, chips), chain_device(c + steps, chips)) for c in range(count - steps)
    ]
    return lax.ppermute(value, "ctx", pairs)


def to_sibling(value):
    count = lax.axis_size("ctx")
    return lax.ppermute(value, "ctx", [(i, i ^ 1) for i in range(count)])


def my_chunks():
    me = lax.axis_index("ctx")
    count = lax.axis_size("ctx")
    core = lax.rem(me, 2)
    chip = lax.div(me, 2)
    low, high = chip, count - 1 - chip
    mine = jnp.where(core == 0, low, high)
    other = jnp.where(core == 0, high, low)
    return core, mine, other


def swap_halves(x):
    return pltpu.roll(x, x.shape[-1] // 2, axis=x.ndim - 1)


def prepare_kernel(half, docs_ref, freq_ref, q_ref, qrot_ref, cos_ref, sin_ref, base_ref, start_ref, work):
    core, mine, other = my_chunks()
    size = 2 * half
    width = freq_ref.shape[-1]
    groups = qrot_ref.shape[1]
    freq = freq_ref[...]
    steps = lax.broadcasted_iota(jnp.int32, (size, width), 0).astype(jnp.float32)
    angle = steps * freq
    cos_ref[...] = jnp.cos(angle)
    sin_ref[...] = jnp.sin(angle)
    row = lax.broadcasted_iota(jnp.int32, (8, width), 0)
    sign = jnp.where(lax.broadcasted_iota(jnp.int32, (1, width), 1) < width // 2, -1.0, 1.0)
    for stream, chunk in enumerate((mine, other)):
        place = ((chunk - row) * size).astype(jnp.float32) * freq
        base_ref[2 * stream] = jnp.cos(place)
        base_ref[2 * stream + 1] = jnp.sin(place)
    docs = docs_ref.shape[0]
    lanes = lax.broadcasted_iota(jnp.int32, (8, half), 1)
    places = [mine * size + lanes, other * size + half + lanes]

    def doc_step(i, carry):
        end, low, high = carry
        end = end + docs_ref[i]
        return (
            end,
            jnp.where(places[0] >= end, end, low),
            jnp.where(places[1] >= end, end, high),
        )

    zero = jnp.zeros((8, half), jnp.int32)
    _, low, high = lax.fori_loop(0, docs, doc_step, (jnp.int32(0), zero, zero))
    start_ref[0] = low
    start_ref[1] = high
    tokens = 16
    heads = q_ref.shape[1]
    per = heads // groups
    for stream in range(2):
        shift = half * stream
        base_cos = base_ref[2 * stream, 0:1, :]
        base_sin = base_ref[2 * stream + 1, 0:1, :]
        c = cos_ref[pl.ds(shift, half), :]
        s = sin_ref[pl.ds(shift, half), :]
        work[0] = (base_cos * c - base_sin * s)[:, None, :]
        work[1] = ((base_sin * c + base_cos * s) * sign)[:, None, :]
        first = jnp.where(core == 0, half * stream, half * (1 - stream))

        def rope_step(i, carry):
            at = i * tokens
            x = q_ref[pl.ds(first + at, tokens)].astype(jnp.float32)
            y = x * work[0, pl.ds(at, tokens)] + swap_halves(x) * work[1, pl.ds(at, tokens)]
            for g in range(groups):
                piece = y[:, g * per:(g + 1) * per, :].reshape(tokens * per, width)
                rows = pl.ds(pl.multiple_of(at * per, tokens * per), tokens * per)
                qrot_ref[stream, g, rows, :] = piece.astype(jnp.bfloat16)
            return carry

        lax.fori_loop(0, half // tokens, rope_step, 0)


def load_keys(chunk_ref, head, first, count, cos_ref, sin_ref, base_ref, stream, step,
              key_at, starts, first_place, query_base, keys, values, at):
    width = cos_ref.shape[-1]
    sign = jnp.where(lax.broadcasted_iota(jnp.int32, (1, width), 1) < width // 2, -1.0, 1.0)
    base_cos = base_ref[2 * stream, step:step + 1, :]
    base_sin = base_ref[2 * stream + 1, step:step + 1, :]
    c = cos_ref[pl.ds(first, count), :]
    s = sin_ref[pl.ds(first, count), :]
    cosine = base_cos * c - base_sin * s
    sine = (base_sin * c + base_cos * s) * sign
    half = starts.shape[-1]
    place = first_place + first + lax.broadcasted_iota(jnp.int32, (count, half), 0)
    query = query_base + lax.broadcasted_iota(jnp.int32, (count, half), 1)
    visible = (place >= starts) & (place <= query)
    hidden = jnp.where(visible, 0.0, HIDDEN).astype(jnp.bfloat16)
    for g in range(chunk_ref.shape[0]):
        k = chunk_ref[g, pl.ds(first, count), :width].astype(jnp.float32)
        keys[g, pl.ds(at, count), :width] = (k * cosine + swap_halves(k) * sine).astype(jnp.bfloat16)
        keys[g, pl.ds(at, count), width:] = hidden
        values[g, pl.ds(at, count), :width] = chunk_ref[g, pl.ds(first, count), width:]


def one_hot_rows(pick, half, per):
    rows = half * per
    token = lax.broadcasted_iota(jnp.int32, (rows, half), 0) // per
    lane = lax.broadcasted_iota(jnp.int32, (rows, half), 1)
    pick[...] = jnp.where(token == lane, 1.0, 0.0).astype(jnp.bfloat16)


def scores_of(q, pick, k):
    return lax.dot_general(
        jnp.concatenate([q, pick], axis=1), k, (((1,), (1,)), ((), ())),
        preferred_element_type=jnp.float32,
    )


def near_kernel(half, factor, qrot_ref, cos_ref, sin_ref, base_ref, start_ref, own0, own1, a0, a1, b0, b1,
                acc_ref, max_ref, keys, values, pick):
    core, mine, other = my_chunks()
    size = 2 * half
    groups, rows, width = qrot_ref.shape[1:]
    per = rows // half
    one_hot_rows(pick, half, per)
    values[:, :, width:] = jnp.ones(values.shape[:2] + (width,), jnp.bfloat16)
    tile = 256
    for stream, chunk, own, own_count, one, two in ((0, mine, own0, half, a0, b0), (1, other, own1, size, a1, b1)):
        starts = start_ref[stream, 0:1, :]
        query_base = chunk * size + half * stream
        at = 0
        for step, ref, count in ((0, own, own_count), (1, one, size), (2, two, size)):
            load_keys(ref, None, 0, count, cos_ref, sin_ref, base_ref, stream, step, None,
                      starts, (chunk - step) * size, query_base, keys, values, at)
            at += count
        for g in range(groups):
            def body(i, carry):
                r = pl.ds(pl.multiple_of(i * tile, tile), tile)
                s = scores_of(qrot_ref[stream, g, r, :], pick[r, :], keys[g, :at, :])
                top = jnp.max(s, axis=1, keepdims=True)
                p = jnp.exp2((s - top) * factor).astype(jnp.bfloat16)
                acc_ref[stream, g, r, :] = jnp.dot(p, values[g, :at, :], preferred_element_type=jnp.float32)
                max_ref[stream, g, r, :] = jnp.broadcast_to(top, (tile, width))
                return carry

            lax.fori_loop(0, rows // tile, body, 0)


def far_kernel(half, factor, qrot_ref, cos_ref, sin_ref, base_ref, start_ref, acc_ref, max_ref, a0, a1, b0, b1,
               out_ref, keys, values, pick):
    core, mine, other = my_chunks()
    size = 2 * half
    groups, rows, width = qrot_ref.shape[1:]
    per = rows // half
    one_hot_rows(pick, half, per)
    values[:, :, width:] = jnp.ones(values.shape[:2] + (width,), jnp.bfloat16)
    tile = 256
    tokens = tile // per
    for stream, chunk, one, two in ((0, mine, a0, b0), (1, other, a1, b1)):
        starts = start_ref[stream, 0:1, :]
        query_base = chunk * size + half * stream
        first_row = jnp.where(core == 0, half * stream, half * (1 - stream))
        need = jnp.min(starts) < (chunk - 2) * size

        @pl.when(need)
        def _():
            at = 0
            for step, ref, first, count in ((3, one, 0, size), (4, two, half * stream, size - half * stream)):
                load_keys(ref, None, first, count, cos_ref, sin_ref, base_ref, stream, step, None,
                          starts, (chunk - step) * size, query_base, keys, values, at)
                at += count

            def body(i, carry):
                r = pl.ds(pl.multiple_of(i * tile, tile), tile)
                parts = []
                for g in range(groups):
                    s = scores_of(qrot_ref[stream, g, r, :], pick[r, :], keys[g, :at, :])
                    before = max_ref[stream, g, r, :]
                    top = jnp.maximum(before, jnp.max(s, axis=1, keepdims=True))
                    p = jnp.exp2((s - top[:, :1]) * factor).astype(jnp.bfloat16)
                    scale = jnp.exp2((before - top) * factor)
                    new = jnp.dot(p, values[g, :at, :], preferred_element_type=jnp.float32)
                    old = acc_ref[stream, g, r, :]
                    o = (old[:, :width] * scale + new[:, :width]) / (old[:, width:] * scale + new[:, width:])
                    parts.append(o.reshape(tokens, per, width))
                out_ref[pl.ds(first_row + i * tokens, tokens)] = jnp.concatenate(parts, axis=1).astype(jnp.bfloat16)
                return carry

            lax.fori_loop(0, rows // tile, body, 0)

        @pl.when(jnp.logical_not(need))
        def _():
            def body(i, carry):
                r = pl.ds(pl.multiple_of(i * tile, tile), tile)
                parts = []
                for g in range(groups):
                    old = acc_ref[stream, g, r, :]
                    parts.append((old[:, :width] / old[:, width:]).reshape(tokens, per, width))
                out_ref[pl.ds(first_row + i * tokens, tokens)] = jnp.concatenate(parts, axis=1).astype(jnp.bfloat16)
                return carry

            lax.fori_loop(0, rows // tile, body, 0)


def shards(key_value, queries, doc_lengths):
    rows, groups, pair = key_value.shape
    width = pair // 2
    half = rows // 2
    heads = queries.shape[1]
    per = heads // groups
    factor = math.log2(math.e) / math.sqrt(width)
    vmem = pl.BlockSpec(memory_space=pltpu.VMEM)
    smem = pl.BlockSpec(memory_space=pltpu.SMEM)
    f32, bf16, i32 = jnp.float32, jnp.bfloat16, jnp.int32

    received = to_sibling(key_value)
    core = lax.rem(lax.axis_index("ctx"), 2)
    first = core * half
    second = (1 - core) * half

    def take(x, start):
        return lax.dynamic_slice_in_dim(x, start, half, 0)

    own = jnp.concatenate([take(key_value, first), take(received, first)], 0).transpose(1, 0, 2)
    own_other = jnp.concatenate([take(received, second), take(key_value, second)], 0).transpose(1, 0, 2)

    index = np.arange(width) % (width // 2)
    freq = jnp.asarray((ROPE_BASE ** (-(index * 2.0 / width))).astype(np.float32)[None, :])

    two = along_chain(own, 2)
    one = along_chain(own, 1)
    four = along_chain(two, 2)
    three = along_chain(one, 2)
    one_other, two_other, three_other, four_other = (to_sibling(x) for x in (one, two, three, four))

    shape = jax.ShapeDtypeStruct
    qrot, cos, sin, base, starts = pl.pallas_call(
        functools.partial(prepare_kernel, half),
        out_shape=(
            shape((2, groups, half * per, width), bf16),
            shape((rows, width), f32),
            shape((rows, width), f32),
            shape((4, 8, width), f32),
            shape((2, 8, half), i32),
        ),
        in_specs=[smem, vmem, vmem],
        out_specs=(vmem,) * 5,
        scratch_shapes=[pltpu.VMEM((2, half, 1, width), f32)],
        cost_estimate=pl.CostEstimate(flops=10 ** 8, bytes_accessed=2 * 10 ** 6, transcendentals=10 ** 5),
        name="prepare",
    )(doc_lengths, freq, queries)

    acc, top = pl.pallas_call(
        functools.partial(near_kernel, half, factor),
        out_shape=(
            shape((2, groups, half * per, 2 * width), f32),
            shape((2, groups, half * per, width), f32),
        ),
        in_specs=[vmem] * 11,
        out_specs=(vmem,) * 2,
        scratch_shapes=[
            pltpu.VMEM((groups, 3 * rows, 2 * width), bf16),
            pltpu.VMEM((groups, 3 * rows, 2 * width), bf16),
            pltpu.VMEM((half * per, half), bf16),
        ],
        cost_estimate=pl.CostEstimate(flops=3 * 10 ** 9, bytes_accessed=6 * 10 ** 6, transcendentals=3 * 10 ** 6),
        name="near",
    )(qrot, cos, sin, base, starts, own, own_other, one, one_other, two, two_other)

    return pl.pallas_call(
        functools.partial(far_kernel, half, factor),
        out_shape=shape((rows, heads, width), bf16),
        in_specs=[vmem] * 11,
        out_specs=vmem,
        scratch_shapes=[
            pltpu.VMEM((groups, 2 * rows, 2 * width), bf16),
            pltpu.VMEM((groups, 2 * rows, 2 * width), bf16),
            pltpu.VMEM((half * per, half), bf16),
        ],
        cost_estimate=pl.CostEstimate(flops=2 * 10 ** 9, bytes_accessed=6 * 10 ** 6, transcendentals=2 * 10 ** 6),
        name="far",
    )(qrot, cos, sin, base, starts, acc, top, three, three_other, four, four_other)


def solution(mesh):
    in_specs = (P("ctx", "tp", None), P("ctx", "tp", None), P())
    out_specs = P("ctx", "tp", None)
    return jax.shard_map(shards, mesh=mesh, in_specs=in_specs, out_specs=out_specs, check_vma=False)
```

```python
import functools
import math

import jax
import jax.numpy as jnp
from jax import lax
from jax.experimental import pallas as pl
from jax.experimental.layout import Layout, with_layout_constraint
from jax.experimental.pallas import tpu as pltpu
from jax.sharding import PartitionSpec as P

ROPE_BASE = 500000.0
HIDDEN = -3.0e38
TILE = 256


def chain_device(chunk, chips):
    return 2 * chunk if chunk < chips else 2 * (2 * chips - 1 - chunk) + 1


def along_chain(value, steps):
    count = lax.axis_size("ctx")
    chips = count // 2
    pairs = [
        (chain_device(c, chips), chain_device(c + steps, chips)) for c in range(count - steps)
    ]
    return lax.ppermute(value, "ctx", pairs)


def to_sibling(value):
    count = lax.axis_size("ctx")
    return lax.ppermute(value, "ctx", [(i, i ^ 1) for i in range(count)])


def my_chunks():
    me = lax.axis_index("ctx")
    count = lax.axis_size("ctx")
    core = lax.rem(me, 2)
    chip = lax.div(me, 2)
    low, high = chip, count - 1 - chip
    mine = jnp.where(core == 0, low, high)
    other = jnp.where(core == 0, high, low)
    return core, (mine, other)


def first_row(core, stream, half):
    return jnp.where(core == 0, half * stream, half * (1 - stream))


def swap_halves(x):
    return pltpu.roll(x, x.shape[-1] // 2, axis=x.ndim - 1)


def load_keys(chunk_ref, first, count, tables, stream, step, chunk, causal, keys, values, at):
    cos_ref, sin_ref, base_ref, start_ref = tables
    size, width = cos_ref.shape
    half = start_ref.shape[-1]
    c = cos_ref[pl.ds(first, count), :]
    s = sin_ref[pl.ds(first, count), :]
    cosine = base_ref[stream, 0, step:step + 1, :] * c - base_ref[stream, 1, step:step + 1, :] * s
    sine = base_ref[stream, 2, step:step + 1, :] * c + base_ref[stream, 3, step:step + 1, :] * s
    offset = lax.broadcasted_iota(jnp.int32, (count, half), 0)
    visible = offset >= start_ref[stream, 0:1, :] - ((chunk - step) * size + first)
    if causal:
        query = lax.broadcasted_iota(jnp.int32, (count, half), 1) + half * stream
        visible = visible & (offset + first <= query)
    hidden = jnp.where(visible, 0.0, HIDDEN).astype(jnp.bfloat16)
    for g in range(keys.shape[0]):
        k = chunk_ref[g, pl.ds(first, count), :width].astype(jnp.float32)
        keys[g, pl.ds(at, count), :width] = (k * cosine + swap_halves(k) * sine).astype(jnp.bfloat16)
        keys[g, pl.ds(at, count), width:] = hidden
        values[g, pl.ds(at, count), :width] = chunk_ref[g, pl.ds(first, count), width:]


def fill_ones(values):
    width = values.shape[-1] // 2
    values[:, :, width:] = jnp.ones(values.shape[:2] + (width,), jnp.bfloat16)


def scores_of(q, pick, k):
    return lax.dot_general(
        jnp.concatenate([q, pick], axis=1), k, (((1,), (1,)), ((), ())),
        preferred_element_type=jnp.float32,
    )


def tables_kernel(half, docs_ref, freq_ref, q_hbm, q_ref, pick, cos_ref, sin_ref, base_ref, start_ref, arrived):
    core, chunks = my_chunks()
    size = 2 * half
    width = freq_ref.shape[-1]
    rows = pick.shape[0]
    per = rows // half
    load = pltpu.make_async_copy(q_hbm, q_ref, arrived)
    load.start()
    freq = freq_ref[...]
    angle = lax.broadcasted_iota(jnp.int32, (size, width), 0).astype(jnp.float32) * freq
    cos_ref[...] = jnp.cos(angle)
    sin_ref[...] = jnp.sin(angle)
    sign = jnp.where(lax.broadcasted_iota(jnp.int32, (1, width), 1) < width // 2, -1.0, 1.0)
    step = lax.broadcasted_iota(jnp.int32, (8, width), 0)
    for stream in range(2):
        place = ((chunks[stream] - step) * size).astype(jnp.float32) * freq
        base_cos = jnp.cos(place)
        base_sin = jnp.sin(place)
        base_ref[stream, 0] = base_cos
        base_ref[stream, 1] = base_sin
        base_ref[stream, 2] = base_sin * sign
        base_ref[stream, 3] = base_cos * sign
    lanes = lax.broadcasted_iota(jnp.int32, (8, half), 1)
    places = [chunks[stream] * size + half * stream + lanes for stream in range(2)]

    def doc_step(i, carry):
        end, first, second = carry
        end = end + docs_ref[i]
        return end, jnp.where(places[0] >= end, end, first), jnp.where(places[1] >= end, end, second)

    zero = jnp.zeros((8, half), jnp.int32)
    _, first, second = lax.fori_loop(0, docs_ref.shape[0], doc_step, (jnp.int32(0), zero, zero))
    start_ref[0] = first
    start_ref[1] = second
    token = lax.broadcasted_iota(jnp.int32, (rows, half), 0) // per
    lane = lax.broadcasted_iota(jnp.int32, (rows, half), 1)
    pick[...] = jnp.where(token == lane, 1.0, 0.0).astype(jnp.bfloat16)
    load.wait()


def begin_kernel(half, factor, q_ref, pick, cos_ref, sin_ref, base_ref, start_ref, own0, own1,
                 qrot_ref, acc0, top0, acc1, top1, work, keys, values):
    core, chunks = my_chunks()
    groups, rows, width = qrot_ref.shape[1:]
    per = rows // half
    fill_ones(values)
    tables = (cos_ref, sin_ref, base_ref, start_ref)
    tokens = 16
    for stream, own, acc, top in ((0, own0, acc0, top0), (1, own1, acc1, top1)):
        c = cos_ref[pl.ds(half * stream, half), :]
        s = sin_ref[pl.ds(half * stream, half), :]
        work[0] = (base_ref[stream, 0, 0:1, :] * c - base_ref[stream, 1, 0:1, :] * s)[:, None, :]
        work[1] = (base_ref[stream, 2, 0:1, :] * c + base_ref[stream, 3, 0:1, :] * s)[:, None, :]
        count = half * (1 + stream)
        load_keys(own, 0, count, tables, stream, 0, chunks[stream], True, keys, values, 0)
        base_row = first_row(core, stream, half)

        def rope_step(i, carry):
            at = i * tokens
            x = q_ref[pl.ds(base_row + at, tokens)].astype(jnp.float32)
            y = x * work[0, pl.ds(at, tokens)] + swap_halves(x) * work[1, pl.ds(at, tokens)]
            for g in range(groups):
                piece = y[:, g * per:(g + 1) * per, :].reshape(tokens * per, width)
                r = pl.ds(pl.multiple_of(at * per, tokens * per), tokens * per)
                qrot_ref[stream, g, r, :] = piece.astype(jnp.bfloat16)
            return carry

        lax.fori_loop(0, half // tokens, rope_step, 0)

        def body(i, carry):
            for u in range(2):
                for g in range(groups):
                    r = pl.ds(pl.multiple_of((2 * i + u) * TILE, TILE), TILE)
                    x = scores_of(qrot_ref[stream, g, r, :], pick[r, :], keys[g, :count, :])
                    high = jnp.max(x, axis=1, keepdims=True)
                    p = jnp.exp2((x - high) * factor).astype(jnp.bfloat16)
                    acc[g, r, :] = jnp.dot(p, values[g, :count, :], preferred_element_type=jnp.float32)
                    top[g, r, :] = jnp.broadcast_to(high, (TILE, width))
            return carry

        lax.fori_loop(0, rows // (2 * TILE), body, 0)


def update(factor, q, pick, k, v, acc, before):
    width = before.shape[-1]
    x = scores_of(q, pick, k)
    top = jnp.maximum(before, jnp.max(x, axis=1, keepdims=True))
    p = jnp.exp2((x - top[:, :1]) * factor).astype(jnp.bfloat16)
    scale = jnp.exp2((before - top) * factor)
    new = jnp.dot(p, v, preferred_element_type=jnp.float32)
    return acc[:, :width] * scale + new[:, :width], acc[:, width:] * scale + new[:, width:], top


def middle_kernel(half, factor, stream, qrot_ref, pick, cos_ref, sin_ref, base_ref, start_ref, old_acc, old_top, pair_ref,
                  acc_ref, top_ref, keys, values):
    core, chunks = my_chunks()
    chunk = chunks[stream]
    size = 2 * half
    groups, rows, width = qrot_ref.shape[1:]
    tables = (cos_ref, sin_ref, base_ref, start_ref)
    earliest = jnp.min(start_ref[stream])

    def work(chunks_used):
        fill_ones(values)
        for n in range(chunks_used):
            load_keys(pair_ref.at[n], 0, size, tables, stream, 1 + n, chunk, False, keys, values, n * size)
        count = chunks_used * size

        def body(i, carry):
            for u in range(2):
                for g in range(groups):
                    r = pl.ds(pl.multiple_of((2 * i + u) * TILE, TILE), TILE)
                    first, second, top = update(
                        factor, qrot_ref[stream, g, r, :], pick[r, :], keys[g, :count, :], values[g, :count, :],
                        old_acc[g, r, :], old_top[g, r, :])
                    acc_ref[g, r, :width] = first
                    acc_ref[g, r, width:] = second
                    top_ref[g, r, :] = top
            return carry

        lax.fori_loop(0, rows // (2 * TILE), body, 0)

    far = earliest < (chunk - 1) * size
    close = earliest < chunk * size
    pl.when(far)(lambda: work(2))
    pl.when(close & jnp.logical_not(far))(lambda: work(1))


def end_kernel(half, factor, stream, qrot_ref, pick, cos_ref, sin_ref, base_ref, start_ref, acc_ref, top_ref, pair_ref, *refs):
    out_hbm, keys, values, result, sent = refs[-5:]
    core, chunks = my_chunks()
    chunk = chunks[stream]
    size = 2 * half
    groups, rows, width = qrot_ref.shape[1:]
    per = rows // half
    tokens = TILE // per
    tables = (cos_ref, sin_ref, base_ref, start_ref)
    earliest = jnp.min(start_ref[stream])
    base_row = first_row(core, stream, half)

    def send(part):
        span = half // 2
        return pltpu.make_async_copy(
            result.at[pl.ds(part * span, span)], out_hbm.at[pl.ds(base_row + part * span, span)], sent.at[part])

    def finish(one):
        def body(i, carry):
            for u in range(2):
                at = 2 * i + u
                r = pl.ds(pl.multiple_of(at * TILE, TILE), TILE)
                parts = []
                for g in range(groups):
                    first, second = one(g, r)
                    parts.append((first / second).reshape(tokens, per, width))
                result[pl.ds(at * tokens, tokens)] = jnp.concatenate(parts, axis=1).astype(jnp.bfloat16)
            send(i).start()
            return carry

        lax.fori_loop(0, rows // (2 * TILE), body, 0)

    def work(chunks_used):
        fill_ones(values)
        used = 0
        for n in range(chunks_used):
            begin = half * stream if n == 1 else 0
            load_keys(pair_ref.at[n], begin, size - begin, tables, stream, 3 + n, chunk, False, keys, values, used)
            used += size - begin

        def one(g, r):
            first, second, _ = update(
                factor, qrot_ref[stream, g, r, :], pick[r, :], keys[g, :used, :], values[g, :used, :],
                acc_ref[g, r, :], top_ref[g, r, :])
            return first, second

        finish(one)

    far = earliest < (chunk - 3) * size
    close = earliest < (chunk - 2) * size
    pl.when(far)(lambda: work(2))
    pl.when(close & jnp.logical_not(far))(lambda: work(1))
    pl.when(jnp.logical_not(close))(lambda: finish(lambda g, r: (acc_ref[g, r, :width], acc_ref[g, r, width:])))
    send(0).wait()
    send(1).wait()


def shards(key_value, queries, doc_lengths):
    rows, groups, pair = key_value.shape
    width = pair // 2
    half = rows // 2
    heads = queries.shape[1]
    per = heads // groups
    factor = math.log2(math.e) / math.sqrt(width)
    vmem = pl.BlockSpec(memory_space=pltpu.VMEM)
    smem = pl.BlockSpec(memory_space=pltpu.SMEM)
    hbm = pl.BlockSpec(memory_space=pltpu.HBM)
    f32, bf16, i32 = jnp.float32, jnp.bfloat16, jnp.int32
    local = pltpu.VMEM
    params = pltpu.CompilerParams(vmem_limit_bytes=16 << 20)

    def near(*values):
        return [pltpu.with_memory_space_constraint(x, pltpu.VMEM) for x in values]

    index = (jnp.arange(width, dtype=jnp.int32) % (width // 2)).astype(f32)
    freq = (ROPE_BASE ** (-(index * 2.0 / width)))[None, :]
    received = with_layout_constraint(to_sibling(key_value), Layout((0, 1, 2)))
    q, *tables = pl.pallas_call(
        functools.partial(tables_kernel, half),
        out_shape=(
            local((rows, heads, width), bf16),
            local((half * per, half), bf16),
            local((rows, width), f32),
            local((rows, width), f32),
            local((2, 4, 8, width), f32),
            local((2, 8, half), i32),
        ),
        in_specs=[smem, vmem, hbm],
        out_specs=(vmem,) * 6,
        scratch_shapes=[pltpu.SemaphoreType.DMA(())],
        cost_estimate=pl.CostEstimate(flops=10 ** 7, bytes_accessed=10 ** 6, transcendentals=10 ** 5),
        compiler_params=params,
        name="tables",
    )(doc_lengths, *near(freq), queries)
    received, q = lax.optimization_barrier((received, q))
    core = lax.rem(lax.axis_index("ctx"), 2)
    first = core * half
    second = (1 - core) * half

    def take(x, start):
        return lax.dynamic_slice_in_dim(x, start, half, 0)

    own = jnp.concatenate([take(key_value, first), take(received, first)], 0).transpose(1, 0, 2)
    own_other = jnp.concatenate([take(received, second), take(key_value, second)], 0).transpose(1, 0, 2)

    one = along_chain(own, 1)
    two = along_chain(own, 2)

    state = (local((groups, half * per, 2 * width), f32), local((groups, half * per, width), f32))
    key_scratch = [pltpu.VMEM((groups, 2 * rows, 2 * width), bf16), pltpu.VMEM((groups, 2 * rows, 2 * width), bf16)]
    qrot, acc0, top0, acc1, top1 = pl.pallas_call(
        functools.partial(begin_kernel, half, factor),
        out_shape=(local((2, groups, half * per, width), bf16),) + state + state,
        in_specs=[vmem] * 8,
        out_specs=(vmem,) * 5,
        scratch_shapes=[
            pltpu.VMEM((2, half, 1, width), f32),
            pltpu.VMEM((groups, rows, 2 * width), bf16),
            pltpu.VMEM((groups, rows, 2 * width), bf16),
        ],
        cost_estimate=pl.CostEstimate(flops=2 * 10 ** 9, bytes_accessed=10 ** 6, transcendentals=10 ** 6),
        compiler_params=params,
        name="begin",
    )(*near(q, *tables, own, own_other))
    tables = [qrot] + tables

    near_pair = jnp.stack([one, two])
    near_pair, acc0, acc1 = lax.optimization_barrier((near_pair, acc0, acc1))
    far_pair = along_chain(near_pair, 2)
    near_other = to_sibling(near_pair)

    def middle(stream, acc, top, keys):
        return pl.pallas_call(
            functools.partial(middle_kernel, half, factor, stream),
            out_shape=state,
            in_specs=[vmem] * 9,
            out_specs=(vmem,) * 2,
            scratch_shapes=key_scratch,
            input_output_aliases={6: 0, 7: 1},
            cost_estimate=pl.CostEstimate(flops=10 ** 9, bytes_accessed=10 ** 6, transcendentals=10 ** 6),
            compiler_params=params,
            name="middle%d" % stream,
        )(*near(*tables, acc, top, keys))

    acc0, top0 = middle(0, acc0, top0, near_pair)
    acc1, top1 = middle(1, acc1, top1, near_other)

    far_pair, acc0, acc1 = lax.optimization_barrier((far_pair, acc0, acc1))
    far_other = to_sibling(far_pair)

    def end(stream, acc, top, keys, *out):
        return pl.pallas_call(
            functools.partial(end_kernel, half, factor, stream),
            out_shape=pltpu.HBM((rows, heads, width), bf16),
            in_specs=[vmem] * 9 + [hbm] * len(out),
            out_specs=hbm,
            scratch_shapes=key_scratch + [pltpu.VMEM((half, heads, width), bf16), pltpu.SemaphoreType.DMA((2,))],
            input_output_aliases={9: 0} if out else {},
            cost_estimate=pl.CostEstimate(flops=10 ** 9, bytes_accessed=10 ** 6, transcendentals=10 ** 6),
            compiler_params=params,
            name="end%d" % stream,
        )(*near(*tables, acc, top, keys), *out)

    out = end(0, acc0, top0, far_pair)
    return end(1, acc1, top1, far_other, out)


def solution(mesh):
    in_specs = (P("ctx", "tp", None), P("ctx", "tp", None), P())
    out_specs = P("ctx", "tp", None)
    return jax.shard_map(shards, mesh=mesh, in_specs=in_specs, out_specs=out_specs, check_vma=False)
```

```python
import functools
import math

import jax
import jax.numpy as jnp
from jax import lax
from jax.experimental import pallas as pl
from jax.experimental.layout import Layout, with_layout_constraint
from jax.experimental.pallas import tpu as pltpu
from jax.sharding import PartitionSpec as P


ROPE_BASE = 500000.0
HIDDEN = -3.0e38
TILE = 256


def chain_device(chunk, chips):
    return 2 * chunk if chunk < chips else 2 * (2 * chips - 1 - chunk) + 1


def along_chain(value, steps):
    count = lax.axis_size("ctx")
    chips = count // 2
    pairs = [
        (chain_device(c, chips), chain_device(c + steps, chips)) for c in range(count - steps)
    ]
    return lax.ppermute(value, "ctx", pairs)


def to_sibling(value):
    count = lax.axis_size("ctx")
    return lax.ppermute(value, "ctx", [(i, i ^ 1) for i in range(count)])


def my_chunks():
    me = lax.axis_index("ctx")
    count = lax.axis_size("ctx")
    core = lax.rem(me, 2)
    chip = lax.div(me, 2)
    low, high = chip, count - 1 - chip
    mine = jnp.where(core == 0, low, high)
    other = jnp.where(core == 0, high, low)
    return core, (mine, other)


def first_row(core, stream, half):
    return jnp.where(core == 0, half * stream, half * (1 - stream))


def swap_halves(x):
    return pltpu.roll(x, x.shape[-1] // 2, axis=x.ndim - 1)


def load_keys(chunk_ref, first, count, tables, stream, step, chunk, causal, keys, values, at):
    cos_ref, sin_ref, base_ref, start_ref = tables
    size, width = cos_ref.shape
    half = start_ref.shape[-1]
    c = cos_ref[pl.ds(first, count), :]
    s = sin_ref[pl.ds(first, count), :]
    cosine = base_ref[stream, 0, step:step + 1, :] * c - base_ref[stream, 1, step:step + 1, :] * s
    sine = base_ref[stream, 2, step:step + 1, :] * c + base_ref[stream, 3, step:step + 1, :] * s
    offset = lax.broadcasted_iota(jnp.int32, (count, half), 0)
    visible = offset >= start_ref[stream, 0:1, :] - ((chunk - step) * size + first)
    if causal:
        query = lax.broadcasted_iota(jnp.int32, (count, half), 1) + half * stream
        visible = visible & (offset + first <= query)
    hidden = jnp.where(visible, 0.0, HIDDEN).astype(jnp.bfloat16)
    for g in range(keys.shape[0]):
        k = chunk_ref[g, pl.ds(first, count), :width].astype(jnp.float32)
        keys[g, pl.ds(at, count), :width] = (k * cosine + swap_halves(k) * sine).astype(jnp.bfloat16)
        keys[g, pl.ds(at, count), width:] = hidden
        values[g, pl.ds(at, count), :width] = chunk_ref[g, pl.ds(first, count), width:]


def fill_ones(values):
    width = values.shape[-1] // 2
    values[:, :, width:] = jnp.ones(values.shape[:2] + (width,), jnp.bfloat16)


def scores_of(q, pick, k):
    return lax.dot_general(
        jnp.concatenate([q, pick], axis=1), k, (((1,), (1,)), ((), ())),
        preferred_element_type=jnp.float32,
    )


def tables_kernel(half, freq_ref, docs_hbm, kv_hbm, q_hbm, kv_ref, q_ref, pick, cos_ref, sin_ref, base_ref, start_ref, docs_ref, arrived):
    _, chunks = my_chunks()
    size = 2 * half
    width = freq_ref.shape[-1]
    rows = pick.shape[0]
    per = rows // half
    loads = [
        pltpu.make_async_copy(docs_hbm, docs_ref, arrived.at[0]),
        pltpu.make_async_copy(kv_hbm, kv_ref, arrived.at[1]),
        pltpu.make_async_copy(q_hbm, q_ref, arrived.at[2]),
    ]
    for load in loads:
        load.start()
    freq = freq_ref[...]
    angle = lax.broadcasted_iota(jnp.int32, (size, width), 0).astype(jnp.float32) * freq
    cos_ref[...] = jnp.cos(angle)
    sin_ref[...] = jnp.sin(angle)
    sign = jnp.where(lax.broadcasted_iota(jnp.int32, (1, width), 1) < width // 2, -1.0, 1.0)
    step = lax.broadcasted_iota(jnp.int32, (8, width), 0)
    for stream in range(2):
        place = ((chunks[stream] - step) * size).astype(jnp.float32) * freq
        base_cos = jnp.cos(place)
        base_sin = jnp.sin(place)
        base_ref[stream, 0] = base_cos
        base_ref[stream, 1] = base_sin
        base_ref[stream, 2] = base_sin * sign
        base_ref[stream, 3] = base_cos * sign
    loads[0].wait()
    lanes = lax.broadcasted_iota(jnp.int32, (8, half), 1)
    places = [chunks[stream] * size + half * stream + lanes for stream in range(2)]

    def doc_step(i, carry):
        end, first, second = carry
        end = end + docs_ref[i]
        return end, jnp.where(places[0] >= end, end, first), jnp.where(places[1] >= end, end, second)

    zero = jnp.zeros((8, half), jnp.int32)
    _, first, second = lax.fori_loop(0, docs_ref.shape[0], doc_step, (jnp.int32(0), zero, zero))
    start_ref[0] = first
    start_ref[1] = second
    token = lax.broadcasted_iota(jnp.int32, (rows, half), 0) // per
    lane = lax.broadcasted_iota(jnp.int32, (rows, half), 1)
    pick[...] = jnp.where(token == lane, 1.0, 0.0).astype(jnp.bfloat16)
    loads[1].wait()
    loads[2].wait()


def begin_kernel(half, factor, q_ref, pick, cos_ref, sin_ref, base_ref, start_ref, own0, own1,
                 qrot_ref, acc0, top0, acc1, top1, work, keys, values):
    core, chunks = my_chunks()
    groups, rows, width = qrot_ref.shape[1:]
    per = rows // half
    fill_ones(values)
    tables = (cos_ref, sin_ref, base_ref, start_ref)
    tokens = 16
    for stream, own, acc, top in ((0, own0, acc0, top0), (1, own1, acc1, top1)):
        c = cos_ref[pl.ds(half * stream, half), :]
        s = sin_ref[pl.ds(half * stream, half), :]
        work[0] = (base_ref[stream, 0, 0:1, :] * c - base_ref[stream, 1, 0:1, :] * s)[:, None, :]
        work[1] = (base_ref[stream, 2, 0:1, :] * c + base_ref[stream, 3, 0:1, :] * s)[:, None, :]
        count = half * (1 + stream)
        load_keys(own, 0, count, tables, stream, 0, chunks[stream], True, keys, values, 0)
        base_row = first_row(core, stream, half)

        def rope_step(i, carry):
            at = i * tokens
            x = q_ref[pl.ds(base_row + at, tokens)].astype(jnp.float32)
            y = x * work[0, pl.ds(at, tokens)] + swap_halves(x) * work[1, pl.ds(at, tokens)]
            for g in range(groups):
                piece = y[:, g * per:(g + 1) * per, :].reshape(tokens * per, width)
                r = pl.ds(pl.multiple_of(at * per, tokens * per), tokens * per)
                qrot_ref[stream, g, r, :] = piece.astype(jnp.bfloat16)
            return carry

        lax.fori_loop(0, half // tokens, rope_step, 0)

        def body(i, carry):
            for u in range(2):
                for g in range(groups):
                    r = pl.ds(pl.multiple_of((2 * i + u) * TILE, TILE), TILE)
                    x = scores_of(qrot_ref[stream, g, r, :], pick[r, :], keys[g, :count, :])
                    p, high = weights_of(x, factor, None)
                    acc[g, r, :] = jnp.dot(p, values[g, :count, :], preferred_element_type=jnp.float32)
                    top[g, r, :] = high
            return carry

        lax.fori_loop(0, rows // (2 * TILE), body, 0)


def weights_of(x, factor, before):
    lanes = 128
    pieces = [x[:, c:c + lanes] for c in range(0, x.shape[1], lanes)]
    top = jnp.max(functools.reduce(jnp.maximum, pieces), axis=1, keepdims=True)
    top = jnp.broadcast_to(top, pieces[0].shape)
    if before is not None:
        top = jnp.maximum(before, top)
    p = jnp.concatenate([jnp.exp2((y - top) * factor).astype(jnp.bfloat16) for y in pieces], axis=1)
    return p, top


def update(factor, q, pick, k, v, acc, before):
    width = before.shape[-1]
    p, top = weights_of(scores_of(q, pick, k), factor, before)
    scale = jnp.exp2((before - top) * factor)
    new = jnp.dot(p, v, preferred_element_type=jnp.float32)
    return acc[:, :width] * scale + new[:, :width], acc[:, width:] * scale + new[:, width:], top


def middle_kernel(half, factor, stream, qrot_ref, pick, cos_ref, sin_ref, base_ref, start_ref, old_acc, old_top, pair_ref,
                  acc_ref, top_ref, keys, values):
    _, chunks = my_chunks()
    chunk = chunks[stream]
    size = 2 * half
    groups, rows, width = qrot_ref.shape[1:]
    tables = (cos_ref, sin_ref, base_ref, start_ref)
    earliest = jnp.min(start_ref[stream])

    def work(chunks_used):
        fill_ones(values)
        for n in range(chunks_used):
            load_keys(pair_ref.at[n], 0, size, tables, stream, 1 + n, chunk, False, keys, values, n * size)
        count = chunks_used * size

        def body(i, carry):
            for u in range(2):
                for g in range(groups):
                    r = pl.ds(pl.multiple_of((2 * i + u) * TILE, TILE), TILE)
                    first, second, top = update(
                        factor, qrot_ref[stream, g, r, :], pick[r, :], keys[g, :count, :], values[g, :count, :],
                        old_acc[g, r, :], old_top[g, r, :])
                    acc_ref[g, r, :width] = first
                    acc_ref[g, r, width:] = second
                    top_ref[g, r, :] = top
            return carry

        lax.fori_loop(0, rows // (2 * TILE), body, 0)

    far = earliest < (chunk - 1) * size
    close = earliest < chunk * size
    pl.when(far)(lambda: work(2))
    pl.when(close & jnp.logical_not(far))(lambda: work(1))


def end_kernel(half, factor, stream, qrot_ref, pick, cos_ref, sin_ref, base_ref, start_ref, acc_ref, top_ref, pair_ref, *refs):
    out_hbm, keys, values, result, sent = refs[-5:]
    core, chunks = my_chunks()
    chunk = chunks[stream]
    size = 2 * half
    groups, rows, width = qrot_ref.shape[1:]
    per = rows // half
    tokens = TILE // per
    tables = (cos_ref, sin_ref, base_ref, start_ref)
    earliest = jnp.min(start_ref[stream])
    base_row = first_row(core, stream, half)

    def send(part):
        span = half // 2
        return pltpu.make_async_copy(
            result.at[pl.ds(part * span, span)], out_hbm.at[pl.ds(base_row + part * span, span)], sent.at[part])

    def finish(one):
        def body(i, carry):
            for u in range(2):
                at = 2 * i + u
                r = pl.ds(pl.multiple_of(at * TILE, TILE), TILE)
                parts = []
                for g in range(groups):
                    first, second = one(g, r)
                    parts.append((first / second).reshape(tokens, per, width))
                result[pl.ds(at * tokens, tokens)] = jnp.concatenate(parts, axis=1).astype(jnp.bfloat16)
            send(i).start()
            return carry

        lax.fori_loop(0, rows // (2 * TILE), body, 0)

    def work(chunks_used):
        fill_ones(values)
        used = 0
        for n in range(chunks_used):
            begin = half * stream if n == 1 else 0
            load_keys(pair_ref.at[n], begin, size - begin, tables, stream, 3 + n, chunk, False, keys, values, used)
            used += size - begin

        def one(g, r):
            first, second, _ = update(
                factor, qrot_ref[stream, g, r, :], pick[r, :], keys[g, :used, :], values[g, :used, :],
                acc_ref[g, r, :], top_ref[g, r, :])
            return first, second

        finish(one)

    far = earliest < (chunk - 3) * size
    close = earliest < (chunk - 2) * size
    pl.when(far)(lambda: work(2))
    pl.when(close & jnp.logical_not(far))(lambda: work(1))
    pl.when(jnp.logical_not(close))(lambda: finish(lambda g, r: (acc_ref[g, r, :width], acc_ref[g, r, width:])))
    send(0).wait()
    send(1).wait()


def shards(key_value, queries, doc_lengths):
    rows, groups, pair = key_value.shape
    width = pair // 2
    half = rows // 2
    heads = queries.shape[1]
    per = heads // groups
    factor = math.log2(math.e) / math.sqrt(width)
    vmem = pl.BlockSpec(memory_space=pltpu.VMEM)
    smem = pl.BlockSpec(memory_space=pltpu.SMEM)
    hbm = pl.BlockSpec(memory_space=pltpu.HBM)
    f32, bf16, i32 = jnp.float32, jnp.bfloat16, jnp.int32
    local = pltpu.VMEM
    params = pltpu.CompilerParams(vmem_limit_bytes=16 << 20)

    def near(*values):
        return [pltpu.with_memory_space_constraint(x, pltpu.VMEM) for x in values]

    def far(*values):
        return [pltpu.with_memory_space_constraint(x, pltpu.HBM) for x in values]

    index = (jnp.arange(width, dtype=jnp.int32) % (width // 2)).astype(f32)
    freq = (ROPE_BASE ** (-(index * 2.0 / width)))[None, :]
    received = with_layout_constraint(to_sibling(key_value), Layout((0, 1, 2)))
    kv, q, *tables = pl.pallas_call(
        functools.partial(tables_kernel, half),
        out_shape=(
            local((rows, groups, pair), bf16),
            local((rows, heads, width), bf16),
            local((half * per, half), bf16),
            local((rows, width), f32),
            local((rows, width), f32),
            local((2, 4, 8, width), f32),
            local((2, 8, half), i32),
        ),
        in_specs=[vmem, hbm, hbm, hbm],
        out_specs=(vmem,) * 7,
        scratch_shapes=[pltpu.SMEM(doc_lengths.shape, i32), pltpu.SemaphoreType.DMA((3,))],
        cost_estimate=pl.CostEstimate(flops=10 ** 7, bytes_accessed=10 ** 6, transcendentals=10 ** 5),
        compiler_params=params,
        name="tables",
    )(*near(freq), *far(doc_lengths, key_value, queries))
    received, kv, q = lax.optimization_barrier((received, kv, q))
    core = lax.rem(lax.axis_index("ctx"), 2)
    first = core * half
    second = (1 - core) * half

    def take(x, start):
        return lax.dynamic_slice_in_dim(x, start, half, 0)

    own = jnp.concatenate([take(kv, first), take(received, first)], 0).transpose(1, 0, 2)
    own_other = jnp.concatenate([take(received, second), take(kv, second)], 0).transpose(1, 0, 2)

    one = along_chain(own, 1)
    two = along_chain(own, 2)

    state = (local((groups, half * per, 2 * width), f32), local((groups, half * per, width), f32))
    key_scratch = [pltpu.VMEM((groups, 2 * rows, 2 * width), bf16), pltpu.VMEM((groups, 2 * rows, 2 * width), bf16)]
    qrot, acc0, top0, acc1, top1 = pl.pallas_call(
        functools.partial(begin_kernel, half, factor),
        out_shape=(local((2, groups, half * per, width), bf16),) + state + state,
        in_specs=[vmem] * 8,
        out_specs=(vmem,) * 5,
        scratch_shapes=[
            pltpu.VMEM((2, half, 1, width), f32),
            pltpu.VMEM((groups, rows, 2 * width), bf16),
            pltpu.VMEM((groups, rows, 2 * width), bf16),
        ],
        cost_estimate=pl.CostEstimate(flops=2 * 10 ** 9, bytes_accessed=10 ** 6, transcendentals=10 ** 6),
        compiler_params=params,
        name="begin",
    )(*near(q, *tables, own, own_other))
    tables = [qrot] + tables

    near_pair = jnp.stack([one, two])
    near_pair, acc0, acc1 = lax.optimization_barrier((near_pair, acc0, acc1))
    far_pair = along_chain(near_pair, 2)
    near_other = to_sibling(near_pair)

    def middle(stream, acc, top, keys):
        return pl.pallas_call(
            functools.partial(middle_kernel, half, factor, stream),
            out_shape=state,
            in_specs=[vmem] * 9,
            out_specs=(vmem,) * 2,
            scratch_shapes=key_scratch,
            input_output_aliases={6: 0, 7: 1},
            cost_estimate=pl.CostEstimate(flops=10 ** 9, bytes_accessed=10 ** 6, transcendentals=10 ** 6),
            compiler_params=params,
        )(*near(*tables, acc, top, keys))

    acc0, top0 = middle(0, acc0, top0, near_pair)
    acc1, top1 = middle(1, acc1, top1, near_other)

    far_pair, acc0, acc1 = lax.optimization_barrier((far_pair, acc0, acc1))
    far_other = to_sibling(far_pair)

    def end(stream, acc, top, keys, *out):
        return pl.pallas_call(
            functools.partial(end_kernel, half, factor, stream),
            out_shape=pltpu.HBM((rows, heads, width), bf16),
            in_specs=[vmem] * 9 + [hbm] * len(out),
            out_specs=hbm,
            scratch_shapes=key_scratch + [pltpu.VMEM((half, heads, width), bf16), pltpu.SemaphoreType.DMA((2,))],
            input_output_aliases={9: 0} if out else {},
            cost_estimate=pl.CostEstimate(flops=10 ** 9, bytes_accessed=10 ** 6, transcendentals=10 ** 6),
            compiler_params=params,
        )(*near(*tables, acc, top, keys), *out)

    out = end(0, acc0, top0, far_pair)
    return end(1, acc1, top1, far_other, out)


def solution(mesh):
    in_specs = (P("ctx", "tp", None), P("ctx", "tp", None), P())
    out_specs = P("ctx", "tp", None)
    return jax.shard_map(shards, mesh=mesh, in_specs=in_specs, out_specs=out_specs, check_vma=False)
```

```python
import functools
import math

import jax
import jax.numpy as jnp
from jax import lax
from jax.experimental import pallas as pl
from jax.experimental.layout import Layout, with_layout_constraint
from jax.experimental.pallas import tpu as pltpu
from jax.sharding import PartitionSpec as P


ROPE_BASE = 500000.0
HIDDEN = -3.0e38
TILE = 256


def chain_device(chunk, chips):
    return 2 * chunk if chunk < chips else 2 * (2 * chips - 1 - chunk) + 1


def along_chain(value, steps):
    count = lax.axis_size("ctx")
    chips = count // 2
    pairs = [
        (chain_device(c, chips), chain_device(c + steps, chips)) for c in range(count - steps)
    ]
    return lax.ppermute(value, "ctx", pairs)


def to_sibling(value):
    count = lax.axis_size("ctx")
    return lax.ppermute(value, "ctx", [(i, i ^ 1) for i in range(count)])


def my_chunks():
    me = lax.axis_index("ctx")
    count = lax.axis_size("ctx")
    core = lax.rem(me, 2)
    chip = lax.div(me, 2)
    low, high = chip, count - 1 - chip
    mine = jnp.where(core == 0, low, high)
    other = jnp.where(core == 0, high, low)
    return core, (mine, other)


def first_row(core, stream, half):
    return jnp.where(core == 0, half * stream, half * (1 - stream))


def swap_halves(x):
    return pltpu.roll(x, x.shape[-1] // 2, axis=x.ndim - 1)


def chunk_rotation(tables, stream, step):
    cos_ref, sin_ref, base_ref, _ = tables
    c = cos_ref[...]
    s = sin_ref[...]
    cosine = base_ref[stream, 0, step:step + 1, :] * c - base_ref[stream, 1, step:step + 1, :] * s
    sine = base_ref[stream, 2, step:step + 1, :] * c + base_ref[stream, 3, step:step + 1, :] * s
    return cosine, sine


def rotate_keys(chunk_ref, g, rotation):
    cosine, sine = rotation
    k = chunk_ref[g, :, :cosine.shape[-1]].astype(jnp.float32)
    return (k * cosine + swap_halves(k) * sine).astype(jnp.bfloat16)


def hide(start_ref, stream, step, chunk, first, count, causal, hidden, at):
    half = start_ref.shape[-1]
    size = 2 * half
    offset = lax.broadcasted_iota(jnp.int32, (count, half), 0)
    visible = offset >= start_ref[stream, 0:1, :] - ((chunk - step) * size + first)
    if causal:
        query = lax.broadcasted_iota(jnp.int32, (count, half), 1) + half * stream
        visible = visible & (offset + first <= query)
    hidden[pl.ds(at, count), :] = jnp.where(visible, 0.0, HIDDEN).astype(jnp.bfloat16)


def masked_keys(pieces, hidden):
    k = jnp.concatenate(pieces, axis=0)
    return jnp.concatenate([k, hidden[:k.shape[0], :]], axis=1)


def counted_values(pieces):
    v = jnp.concatenate(pieces, axis=0)
    return jnp.concatenate([v, jnp.ones_like(v)], axis=1)


def scores_of(q, pick, k):
    return lax.dot_general(
        jnp.concatenate([q, pick], axis=1), k, (((1,), (1,)), ((), ())),
        preferred_element_type=jnp.float32,
    )


def tables_kernel(half, freq_ref, docs_hbm, kv_hbm, q_hbm, kv_ref, q_ref, pick, cos_ref, sin_ref, base_ref, start_ref, docs_ref, arrived):
    _, chunks = my_chunks()
    size = 2 * half
    width = freq_ref.shape[-1]
    rows = pick.shape[0]
    per = rows // half
    loads = [
        pltpu.make_async_copy(docs_hbm, docs_ref, arrived.at[0]),
        pltpu.make_async_copy(kv_hbm, kv_ref, arrived.at[1]),
        pltpu.make_async_copy(q_hbm, q_ref, arrived.at[2]),
    ]
    for load in loads:
        load.start()
    freq = freq_ref[...]
    angle = lax.broadcasted_iota(jnp.int32, (size, width), 0).astype(jnp.float32) * freq
    cos_ref[...] = jnp.cos(angle)
    sin_ref[...] = jnp.sin(angle)
    sign = jnp.where(lax.broadcasted_iota(jnp.int32, (1, width), 1) < width // 2, -1.0, 1.0)
    step = lax.broadcasted_iota(jnp.int32, (8, width), 0)
    for stream in range(2):
        place = ((chunks[stream] - step) * size).astype(jnp.float32) * freq
        base_cos = jnp.cos(place)
        base_sin = jnp.sin(place)
        base_ref[stream, 0] = base_cos
        base_ref[stream, 1] = base_sin
        base_ref[stream, 2] = base_sin * sign
        base_ref[stream, 3] = base_cos * sign
    loads[0].wait()
    lanes = lax.broadcasted_iota(jnp.int32, (8, half), 1)
    places = [chunks[stream] * size + half * stream + lanes for stream in range(2)]

    def doc_step(i, carry):
        end, first, second = carry
        end = end + docs_ref[i]
        return end, jnp.where(places[0] >= end, end, first), jnp.where(places[1] >= end, end, second)

    zero = jnp.zeros((8, half), jnp.int32)
    _, first, second = lax.fori_loop(0, docs_ref.shape[0], doc_step, (jnp.int32(0), zero, zero))
    start_ref[0] = first
    start_ref[1] = second
    token = lax.broadcasted_iota(jnp.int32, (rows, half), 0) // per
    lane = lax.broadcasted_iota(jnp.int32, (rows, half), 1)
    pick[...] = jnp.where(token == lane, 1.0, 0.0).astype(jnp.bfloat16)
    loads[1].wait()
    loads[2].wait()


def rotate_kernel(chunk_ref, cos_ref, sin_ref, base_ref, out_ref):
    width = cos_ref.shape[-1]
    rotation = chunk_rotation((cos_ref, sin_ref, base_ref, None), 0, 0)
    for g in range(chunk_ref.shape[0]):
        out_ref[g, :, :width] = rotate_keys(chunk_ref, g, rotation)
        out_ref[g, :, width:] = chunk_ref[g, :, width:]


def begin_kernel(half, factor, stream, q_ref, pick, cos_ref, sin_ref, base_ref, start_ref, own,
                 qrot_ref, acc, top, work, keys, hidden):
    core, chunks = my_chunks()
    groups, rows, width = qrot_ref.shape
    per = rows // half
    tables = (cos_ref, sin_ref, base_ref, start_ref)
    tokens = 16
    c = cos_ref[pl.ds(half * stream, half), :]
    s = sin_ref[pl.ds(half * stream, half), :]
    work[0] = (base_ref[stream, 0, 0:1, :] * c - base_ref[stream, 1, 0:1, :] * s)[:, None, :]
    work[1] = (base_ref[stream, 2, 0:1, :] * c + base_ref[stream, 3, 0:1, :] * s)[:, None, :]
    count = half * (1 + stream)
    hide(start_ref, stream, 0, chunks[stream], 0, count, True, hidden, 0)
    if stream == 1:
        rotation = chunk_rotation(tables, 1, 0)
        for g in range(groups):
            keys[g] = rotate_keys(own, g, rotation)
    base_row = first_row(core, stream, half)

    def rope_step(i, carry):
        at = i * tokens
        x = q_ref[pl.ds(base_row + at, tokens)].astype(jnp.float32)
        y = x * work[0, pl.ds(at, tokens)] + swap_halves(x) * work[1, pl.ds(at, tokens)]
        for g in range(groups):
            piece = y[:, g * per:(g + 1) * per, :].reshape(tokens * per, width)
            r = pl.ds(pl.multiple_of(at * per, tokens * per), tokens * per)
            qrot_ref[g, r, :] = piece.astype(jnp.bfloat16)
        return carry

    lax.fori_loop(0, half // tokens, rope_step, 0)

    def body(i, carry):
        for u in range(2):
            for g in range(groups):
                r = pl.ds(pl.multiple_of((2 * i + u) * TILE, TILE), TILE)
                k = keys[g] if stream == 1 else own[g, :count, :width]
                x = scores_of(qrot_ref[g, r, :], pick[r, :], masked_keys([k], hidden))
                p, high = weights_of(x, factor, None)
                v = counted_values([own[g, :count, width:]])
                acc[g, r, :] = jnp.dot(p, v, preferred_element_type=jnp.float32)
                top[g, r, :] = high
        return carry

    lax.fori_loop(0, rows // (2 * TILE), body, 0)


def weights_of(x, factor, before):
    lanes = 128
    pieces = [x[:, c:c + lanes] for c in range(0, x.shape[1], lanes)]
    top = jnp.max(functools.reduce(jnp.maximum, pieces), axis=1, keepdims=True)
    top = jnp.broadcast_to(top, pieces[0].shape)
    if before is not None:
        top = jnp.maximum(before, top)
    p = jnp.concatenate([jnp.exp2((y - top) * factor).astype(jnp.bfloat16) for y in pieces], axis=1)
    return p, top


def update(factor, q, pick, k, v, acc, before):
    width = before.shape[-1]
    p, top = weights_of(scores_of(q, pick, k), factor, before)
    scale = jnp.exp2((before - top) * factor)
    new = jnp.dot(p, v, preferred_element_type=jnp.float32)
    return acc[:, :width] * scale + new[:, :width], acc[:, width:] * scale + new[:, width:], top


def seeing(start_ref, stream, place, iterations):
    starts = start_ref[stream]
    span = starts.shape[-1] // iterations
    lane = lax.broadcasted_iota(jnp.int32, starts.shape, 1)
    reached = jnp.where((starts < place) & (lane % span == 0), 1, 0)
    return lax.div(jnp.sum(reached), starts.shape[0])


def middle_kernel(half, factor, stream, qrot_ref, pick, cos_ref, sin_ref, base_ref, start_ref, old_acc, old_top, pair_ref,
                  acc_ref, top_ref, hidden):
    _, chunks = my_chunks()
    chunk = chunks[stream]
    size = 2 * half
    groups, rows, width = qrot_ref.shape
    iterations = rows // (2 * TILE)

    def work(chunks_used, low, high):
        def piece(g, lanes):
            return [pair_ref[n, g, :, lanes] for n in range(chunks_used)]

        def body(i, carry):
            for u in range(2):
                for g in range(groups):
                    r = pl.ds(pl.multiple_of((2 * i + u) * TILE, TILE), TILE)
                    first, second, top = update(
                        factor, qrot_ref[g, r, :], pick[r, :], masked_keys(piece(g, slice(0, width)), hidden),
                        counted_values(piece(g, slice(width, None))), old_acc[g, r, :], old_top[g, r, :])
                    acc_ref[g, r, :width] = first
                    acc_ref[g, r, width:] = second
                    top_ref[g, r, :] = top
            return carry

        lax.fori_loop(low, high, body, 0)

    close = seeing(start_ref, stream, chunk * size, iterations)
    far = seeing(start_ref, stream, (chunk - 1) * size, iterations)

    @pl.when(close > 0)
    def _():
        hide(start_ref, stream, 1, chunk, 0, size, False, hidden, 0)

        @pl.when(far > 0)
        def _():
            hide(start_ref, stream, 2, chunk, 0, size, False, hidden, size)
            work(2, 0, far)

        work(1, far, close)


def end_kernel(half, factor, stream, qrot_ref, pick, cos_ref, sin_ref, base_ref, start_ref, acc_ref, top_ref, pair_ref, *refs):
    out_hbm, hidden, result, sent = refs[-4:]
    core, chunks = my_chunks()
    chunk = chunks[stream]
    size = 2 * half
    groups, rows, width = qrot_ref.shape
    per = rows // half
    tokens = TILE // per
    iterations = rows // (2 * TILE)
    base_row = first_row(core, stream, half)

    def send(part):
        span = half // 2
        return pltpu.make_async_copy(
            result.at[pl.ds(part * span, span)], out_hbm.at[pl.ds(base_row + part * span, span)], sent.at[part])

    def finish(one, low, high):
        def body(i, carry):
            for u in range(2):
                at = 2 * i + u
                r = pl.ds(pl.multiple_of(at * TILE, TILE), TILE)
                parts = []
                for g in range(groups):
                    first, second = one(g, r)
                    parts.append((first / second).reshape(tokens, per, width))
                result[pl.ds(at * tokens, tokens)] = jnp.concatenate(parts, axis=1).astype(jnp.bfloat16)
            send(i).start()
            return carry

        lax.fori_loop(low, high, body, 0)

    begin = half * stream

    def work(spans, low, high):
        def piece(g, lanes):
            return [pair_ref[n, g, span, lanes] for n, span in enumerate(spans)]

        def one(g, r):
            first, second, _ = update(
                factor, qrot_ref[g, r, :], pick[r, :], masked_keys(piece(g, slice(0, width)), hidden),
                counted_values(piece(g, slice(width, None))), acc_ref[g, r, :], top_ref[g, r, :])
            return first, second

        finish(one, low, high)

    close = seeing(start_ref, stream, (chunk - 2) * size, iterations)
    far = seeing(start_ref, stream, (chunk - 3) * size, iterations)

    @pl.when(close > 0)
    def _():
        hide(start_ref, stream, 3, chunk, 0, size, False, hidden, 0)

        @pl.when(far > 0)
        def _():
            hide(start_ref, stream, 4, chunk, begin, size - begin, False, hidden, size)
            work((slice(0, size), slice(begin, size)), 0, far)

        work((slice(0, size),), far, close)

    finish(lambda g, r: (acc_ref[g, r, :width], acc_ref[g, r, width:]), close, iterations)
    send(0).wait()
    send(1).wait()


def shards(key_value, queries, doc_lengths):
    rows, groups, pair = key_value.shape
    width = pair // 2
    half = rows // 2
    heads = queries.shape[1]
    per = heads // groups
    factor = math.log2(math.e) / math.sqrt(width)
    vmem = pl.BlockSpec(memory_space=pltpu.VMEM)
    smem = pl.BlockSpec(memory_space=pltpu.SMEM)
    hbm = pl.BlockSpec(memory_space=pltpu.HBM)
    f32, bf16, i32 = jnp.float32, jnp.bfloat16, jnp.int32
    local = pltpu.VMEM
    params = pltpu.CompilerParams(vmem_limit_bytes=16 << 20)

    def near(*values):
        return [pltpu.with_memory_space_constraint(x, pltpu.VMEM) for x in values]

    def far(*values):
        return [pltpu.with_memory_space_constraint(x, pltpu.HBM) for x in values]

    index = (jnp.arange(width, dtype=jnp.int32) % (width // 2)).astype(f32)
    freq = (ROPE_BASE ** (-(index * 2.0 / width)))[None, :]
    received = with_layout_constraint(to_sibling(key_value), Layout((0, 1, 2)))
    kv, q, *tables = pl.pallas_call(
        functools.partial(tables_kernel, half),
        out_shape=(
            local((rows, groups, pair), bf16),
            local((rows, heads, width), bf16),
            local((half * per, half), bf16),
            local((rows, width), f32),
            local((rows, width), f32),
            local((2, 4, 8, width), f32),
            local((2, 8, half), i32),
        ),
        in_specs=[vmem, hbm, hbm, hbm],
        out_specs=(vmem,) * 7,
        scratch_shapes=[pltpu.SMEM(doc_lengths.shape, i32), pltpu.SemaphoreType.DMA((3,))],
        cost_estimate=pl.CostEstimate(flops=10 ** 7, bytes_accessed=10 ** 6, transcendentals=10 ** 5),
        compiler_params=params,
        name="tables",
    )(*near(freq), *far(doc_lengths, key_value, queries))
    received, kv, q = lax.optimization_barrier((received, kv, q))
    core = lax.rem(lax.axis_index("ctx"), 2)
    first = core * half
    second = (1 - core) * half

    def take(x, start):
        return lax.dynamic_slice_in_dim(x, start, half, 0)

    own = jnp.concatenate([take(kv, first), take(received, first)], 0).transpose(1, 0, 2)
    own_other = jnp.concatenate([take(received, second), take(kv, second)], 0).transpose(1, 0, 2)

    own = pl.pallas_call(
        rotate_kernel,
        out_shape=local((groups, rows, pair), bf16),
        in_specs=[vmem] * 4,
        out_specs=vmem,
        cost_estimate=pl.CostEstimate(flops=10 ** 6, bytes_accessed=10 ** 6, transcendentals=0),
        compiler_params=params,
        name="rotate",
    )(*near(own, *tables[1:4]))

    one = along_chain(own, 1)
    two = along_chain(own, 2)

    state = (local((groups, half * per, 2 * width), f32), local((groups, half * per, width), f32))
    key_scratch = [pltpu.VMEM((2 * rows, half), bf16)]

    def begin(stream, own_keys):
        return pl.pallas_call(
            functools.partial(begin_kernel, half, factor, stream),
            out_shape=(local((groups, half * per, width), bf16),) + state,
            in_specs=[vmem] * 7,
            out_specs=(vmem,) * 3,
            scratch_shapes=[
                pltpu.VMEM((2, half, 1, width), f32),
                pltpu.VMEM((groups, rows, width), bf16),
                pltpu.VMEM((rows, half), bf16),
            ],
            cost_estimate=pl.CostEstimate(flops=10 ** 9, bytes_accessed=10 ** 6, transcendentals=10 ** 6),
            compiler_params=params,
        )(*near(q, *tables, own_keys))

    qrot0, acc0, top0 = begin(0, own)
    qrot1, acc1, top1 = begin(1, own_other)
    near_pair = jnp.stack([one, two])
    near_pair, acc0, acc1 = lax.optimization_barrier((near_pair, acc0, acc1))
    far_pair = along_chain(near_pair, 2)

    def middle(stream, qrot, acc, top, keys):
        return pl.pallas_call(
            functools.partial(middle_kernel, half, factor, stream),
            out_shape=state,
            in_specs=[vmem] * 9,
            out_specs=(vmem,) * 2,
            scratch_shapes=key_scratch,
            input_output_aliases={6: 0, 7: 1},
            cost_estimate=pl.CostEstimate(flops=10 ** 9, bytes_accessed=10 ** 6, transcendentals=10 ** 6),
            compiler_params=params,
        )(*near(qrot, *tables, acc, top, keys))

    acc0, top0 = middle(0, qrot0, acc0, top0, near_pair)
    near_pair, acc0 = lax.optimization_barrier((near_pair, acc0))
    near_other = to_sibling(near_pair)
    acc1, top1 = middle(1, qrot1, acc1, top1, near_other)

    far_pair, acc0, acc1 = lax.optimization_barrier((far_pair, acc0, acc1))
    far_other = to_sibling(far_pair)

    def end(stream, qrot, acc, top, keys, *out):
        return pl.pallas_call(
            functools.partial(end_kernel, half, factor, stream),
            out_shape=pltpu.HBM((rows, heads, width), bf16),
            in_specs=[vmem] * 9 + [hbm] * len(out),
            out_specs=hbm,
            scratch_shapes=key_scratch + [pltpu.VMEM((half, heads, width), bf16), pltpu.SemaphoreType.DMA((2,))],
            input_output_aliases={9: 0} if out else {},
            cost_estimate=pl.CostEstimate(flops=10 ** 9, bytes_accessed=10 ** 6, transcendentals=10 ** 6),
            compiler_params=params,
        )(*near(qrot, *tables, acc, top, keys), *out)

    out = end(0, qrot0, acc0, top0, far_pair)
    return end(1, qrot1, acc1, top1, far_other, out)


def solution(mesh):
    in_specs = (P("ctx", "tp", None), P("ctx", "tp", None), P())
    out_specs = P("ctx", "tp", None)
    return jax.shard_map(shards, mesh=mesh, in_specs=in_specs, out_specs=out_specs, check_vma=False)
```

```python
import functools
import math

import jax
import jax.numpy as jnp
from jax import lax
from jax.experimental import pallas as pl
from jax.experimental.layout import Layout, with_layout_constraint
from jax.experimental.pallas import tpu as pltpu
from jax.sharding import PartitionSpec as P


ROPE_BASE = 500000.0
HIDDEN = -3.0e38
TILE = 256


def chain_device(chunk, chips):
    return 2 * chunk if chunk < chips else 2 * (2 * chips - 1 - chunk) + 1


def along_chain(value, steps):
    count = lax.axis_size("ctx")
    chips = count // 2
    pairs = [
        (chain_device(c, chips), chain_device(c + steps, chips)) for c in range(count - steps)
    ]
    return lax.ppermute(value, "ctx", pairs)


def to_sibling(value):
    count = lax.axis_size("ctx")
    return lax.ppermute(value, "ctx", [(i, i ^ 1) for i in range(count)])


def my_chunks():
    me = lax.axis_index("ctx")
    count = lax.axis_size("ctx")
    core = lax.rem(me, 2)
    chip = lax.div(me, 2)
    low, high = chip, count - 1 - chip
    mine = jnp.where(core == 0, low, high)
    other = jnp.where(core == 0, high, low)
    return core, (mine, other)


def first_row(core, stream, half):
    return jnp.where(core == 0, half * stream, half * (1 - stream))


def swap_halves(x):
    return pltpu.roll(x, x.shape[-1] // 2, axis=x.ndim - 1)


def chunk_rotation(tables, stream, step):
    cos_ref, sin_ref, base_ref, _ = tables
    c = cos_ref[...]
    s = sin_ref[...]
    cosine = base_ref[stream, 0, step:step + 1, :] * c - base_ref[stream, 1, step:step + 1, :] * s
    sine = base_ref[stream, 2, step:step + 1, :] * c + base_ref[stream, 3, step:step + 1, :] * s
    return cosine, sine


def rotate_keys(chunk_ref, g, rotation):
    cosine, sine = rotation
    k = chunk_ref[g, :, :cosine.shape[-1]].astype(jnp.float32)
    return (k * cosine + swap_halves(k) * sine).astype(jnp.bfloat16)


def hide(start_ref, stream, step, chunk, first, count, causal, hidden, at):
    half = start_ref.shape[-1]
    size = 2 * half
    offset = lax.broadcasted_iota(jnp.int32, (count, half), 0)
    visible = offset >= start_ref[stream, 0:1, :] - ((chunk - step) * size + first)
    if causal:
        query = lax.broadcasted_iota(jnp.int32, (count, half), 1) + half * stream
        visible = visible & (offset + first <= query)
    hidden[pl.ds(at, count), :] = jnp.where(visible, 0.0, HIDDEN).astype(jnp.bfloat16)


def masked_keys(pieces, hidden):
    k = jnp.concatenate(pieces, axis=0)
    return jnp.concatenate([k, hidden[:k.shape[0], :]], axis=1)


def counted_values(pieces):
    v = jnp.concatenate(pieces, axis=0)
    return jnp.concatenate([v, jnp.ones_like(v)], axis=1)


def scores_of(q, pick, k):
    return lax.dot_general(
        jnp.concatenate([q, pick], axis=1), k, (((1,), (1,)), ((), ())),
        preferred_element_type=jnp.float32,
    )


def tables_kernel(half, freq_ref, docs_hbm, kv_hbm, q_hbm, kv_ref, q_ref, pick, cos_ref, sin_ref, base_ref, start_ref, docs_ref, arrived):
    _, chunks = my_chunks()
    size = 2 * half
    width = freq_ref.shape[-1]
    rows = pick.shape[0]
    per = rows // half
    loads = [
        pltpu.make_async_copy(docs_hbm, docs_ref, arrived.at[0]),
        pltpu.make_async_copy(kv_hbm, kv_ref, arrived.at[1]),
        pltpu.make_async_copy(q_hbm, q_ref, arrived.at[2]),
    ]
    for load in loads:
        load.start()
    freq = freq_ref[...]
    angle = lax.broadcasted_iota(jnp.int32, (size, width), 0).astype(jnp.float32) * freq
    cos_ref[...] = jnp.cos(angle)
    sin_ref[...] = jnp.sin(angle)
    sign = jnp.where(lax.broadcasted_iota(jnp.int32, (1, width), 1) < width // 2, -1.0, 1.0)
    step = lax.broadcasted_iota(jnp.int32, (8, width), 0)
    for stream in range(2):
        place = ((chunks[stream] - step) * size).astype(jnp.float32) * freq
        base_cos = jnp.cos(place)
        base_sin = jnp.sin(place)
        base_ref[stream, 0] = base_cos
        base_ref[stream, 1] = base_sin
        base_ref[stream, 2] = base_sin * sign
        base_ref[stream, 3] = base_cos * sign
    loads[0].wait()
    lanes = lax.broadcasted_iota(jnp.int32, (8, half), 1)
    places = [chunks[stream] * size + half * stream + lanes for stream in range(2)]

    def doc_step(i, carry):
        end, first, second = carry
        end = end + docs_ref[i]
        return end, jnp.where(places[0] >= end, end, first), jnp.where(places[1] >= end, end, second)

    zero = jnp.zeros((8, half), jnp.int32)
    _, first, second = lax.fori_loop(0, docs_ref.shape[0], doc_step, (jnp.int32(0), zero, zero))
    start_ref[0] = first
    start_ref[1] = second
    token = lax.broadcasted_iota(jnp.int32, (rows, half), 0) // per
    lane = lax.broadcasted_iota(jnp.int32, (rows, half), 1)
    pick[...] = jnp.where(token == lane, 1.0, 0.0).astype(jnp.bfloat16)
    loads[1].wait()
    loads[2].wait()


def rotate_kernel(chunk_ref, cos_ref, sin_ref, base_ref, out_ref):
    width = cos_ref.shape[-1]
    rotation = chunk_rotation((cos_ref, sin_ref, base_ref, None), 0, 0)
    for g in range(chunk_ref.shape[0]):
        out_ref[g, :, :width] = rotate_keys(chunk_ref, g, rotation)
        out_ref[g, :, width:] = chunk_ref[g, :, width:]


def begin_kernel(half, factor, stream, q_ref, pick, cos_ref, sin_ref, base_ref, start_ref, own,
                 qrot_ref, acc, top, work, keys, hidden):
    core, chunks = my_chunks()
    groups, rows, width = qrot_ref.shape
    per = rows // half
    tables = (cos_ref, sin_ref, base_ref, start_ref)
    tokens = 16
    c = cos_ref[pl.ds(half * stream, half), :]
    s = sin_ref[pl.ds(half * stream, half), :]
    work[0] = (base_ref[stream, 0, 0:1, :] * c - base_ref[stream, 1, 0:1, :] * s)[:, None, :]
    work[1] = (base_ref[stream, 2, 0:1, :] * c + base_ref[stream, 3, 0:1, :] * s)[:, None, :]
    count = half * (1 + stream)
    hide(start_ref, stream, 0, chunks[stream], 0, count, True, hidden, 0)
    if stream == 1:
        rotation = chunk_rotation(tables, 1, 0)
        for g in range(groups):
            keys[g] = rotate_keys(own, g, rotation)
    base_row = first_row(core, stream, half)

    def rope_step(i, carry):
        at = i * tokens
        x = q_ref[pl.ds(base_row + at, tokens)].astype(jnp.float32)
        y = x * work[0, pl.ds(at, tokens)] + swap_halves(x) * work[1, pl.ds(at, tokens)]
        for g in range(groups):
            piece = y[:, g * per:(g + 1) * per, :].reshape(tokens * per, width)
            r = pl.ds(pl.multiple_of(at * per, tokens * per), tokens * per)
            qrot_ref[g, r, :] = piece.astype(jnp.bfloat16)
        return carry

    lax.fori_loop(0, half // tokens, rope_step, 0)

    def body(i, carry):
        for u in range(2):
            for g in range(groups):
                r = pl.ds(pl.multiple_of((2 * i + u) * TILE, TILE), TILE)
                k = keys[g] if stream == 1 else own[g, :count, :width]
                x = scores_of(qrot_ref[g, r, :], pick[r, :], masked_keys([k], hidden))
                p, high = weights_of(x, factor, None)
                v = counted_values([own[g, :count, width:]])
                acc[g, r, :] = jnp.dot(p, v, preferred_element_type=jnp.float32)
                top[g, r, :] = high
        return carry

    lax.fori_loop(0, rows // (2 * TILE), body, 0)


def weights_of(x, factor, before):
    lanes = 128
    pieces = [x[:, c:c + lanes] for c in range(0, x.shape[1], lanes)]
    top = jnp.max(functools.reduce(jnp.maximum, pieces), axis=1, keepdims=True)
    top = jnp.broadcast_to(top, pieces[0].shape)
    if before is not None:
        top = jnp.maximum(before, top)
    p = jnp.concatenate([jnp.exp2((y - top) * factor).astype(jnp.bfloat16) for y in pieces], axis=1)
    return p, top


def update(factor, q, pick, k, v, acc, before):
    width = before.shape[-1]
    p, top = weights_of(scores_of(q, pick, k), factor, before)
    scale = jnp.exp2((before - top) * factor)
    new = jnp.dot(p, v, preferred_element_type=jnp.float32)
    return acc[:, :width] * scale + new[:, :width], acc[:, width:] * scale + new[:, width:], top


def seeing(start_ref, stream, place, iterations):
    starts = start_ref[stream]
    span = starts.shape[-1] // iterations
    lane = lax.broadcasted_iota(jnp.int32, starts.shape, 1)
    reached = jnp.where((starts < place) & (lane % span == 0), 1, 0)
    return lax.div(jnp.sum(reached), starts.shape[0])


def middle_kernel(half, factor, stream, qrot_ref, pick, cos_ref, sin_ref, base_ref, start_ref, old_acc, old_top, pair_ref,
                  acc_ref, top_ref, hidden):
    _, chunks = my_chunks()
    chunk = chunks[stream]
    size = 2 * half
    groups, rows, width = qrot_ref.shape
    iterations = rows // (2 * TILE)

    def work(chunks_used, low, high):
        def piece(g, lanes):
            return [pair_ref[n, g, :, lanes] for n in range(chunks_used)]

        def body(i, carry):
            for u in range(2):
                for g in range(groups):
                    r = pl.ds(pl.multiple_of((2 * i + u) * TILE, TILE), TILE)
                    first, second, top = update(
                        factor, qrot_ref[g, r, :], pick[r, :], masked_keys(piece(g, slice(0, width)), hidden),
                        counted_values(piece(g, slice(width, None))), old_acc[g, r, :], old_top[g, r, :])
                    acc_ref[g, r, :width] = first
                    acc_ref[g, r, width:] = second
                    top_ref[g, r, :] = top
            return carry

        lax.fori_loop(low, high, body, 0)

    close = seeing(start_ref, stream, chunk * size, iterations)
    far = seeing(start_ref, stream, (chunk - 1) * size, iterations)

    @pl.when(close > 0)
    def _():
        hide(start_ref, stream, 1, chunk, 0, size, False, hidden, 0)

        @pl.when(far > 0)
        def _():
            hide(start_ref, stream, 2, chunk, 0, size, False, hidden, size)
            work(2, 0, far)

        work(1, far, close)


def end_kernel(half, factor, stream, qrot_ref, pick, cos_ref, sin_ref, base_ref, start_ref, acc_ref, top_ref, far_ref, *refs):
    if stream == 0:
        result, hidden = refs
    else:
        ready, out_hbm, hidden, result, sent = refs
    core, chunks = my_chunks()
    chunk = chunks[stream]
    size = 2 * half
    groups, rows, width = qrot_ref.shape
    per = rows // half
    tokens = TILE // per
    iterations = rows // (2 * TILE)
    span = half // iterations

    def send(part):
        row = first_row(core, 1, half) + part * span
        return pltpu.make_async_copy(result.at[pl.ds(part * span, span)], out_hbm.at[pl.ds(row, span)], sent.at[part])

    if stream == 1:
        earlier = pltpu.make_async_copy(
            ready, out_hbm.at[pl.ds(first_row(core, 0, half), half)], sent.at[iterations])
        earlier.start()

    def finish(one, low, high):
        def body(i, carry):
            for u in range(2):
                at = 2 * i + u
                r = pl.ds(pl.multiple_of(at * TILE, TILE), TILE)
                parts = []
                for g in range(groups):
                    first, second = one(g, r)
                    parts.append((first / second).reshape(tokens, per, width))
                result[pl.ds(at * tokens, tokens)] = jnp.concatenate(parts, axis=1).astype(jnp.bfloat16)
            if stream == 1:
                send(i).start()
            return carry

        lax.fori_loop(low, high, body, 0)

    begin = half * stream

    def work(count, low, high):
        def piece(g, lanes):
            return [far_ref[g, :count, lanes]]

        def one(g, r):
            first, second, _ = update(
                factor, qrot_ref[g, r, :], pick[r, :], masked_keys(piece(g, slice(0, width)), hidden),
                counted_values(piece(g, slice(width, None))), acc_ref[g, r, :], top_ref[g, r, :])
            return first, second

        finish(one, low, high)

    close = seeing(start_ref, stream, (chunk - 2) * size, iterations)
    far = seeing(start_ref, stream, (chunk - 3) * size, iterations)

    @pl.when(close > 0)
    def _():
        hide(start_ref, stream, 3, chunk, 0, size, False, hidden, 0)

        @pl.when(far > 0)
        def _():
            hide(start_ref, stream, 4, chunk, begin, size - begin, False, hidden, size)
            work(2 * size - begin, 0, far)

        work(size, far, close)

    finish(lambda g, r: (acc_ref[g, r, :width], acc_ref[g, r, width:]), close, iterations)
    if stream == 1:
        for part in range(iterations):
            send(part).wait()
        earlier.wait()


def shards(key_value, queries, doc_lengths):
    rows, groups, pair = key_value.shape
    width = pair // 2
    half = rows // 2
    heads = queries.shape[1]
    per = heads // groups
    factor = math.log2(math.e) / math.sqrt(width)
    vmem = pl.BlockSpec(memory_space=pltpu.VMEM)
    smem = pl.BlockSpec(memory_space=pltpu.SMEM)
    hbm = pl.BlockSpec(memory_space=pltpu.HBM)
    f32, bf16, i32 = jnp.float32, jnp.bfloat16, jnp.int32
    local = pltpu.VMEM
    params = pltpu.CompilerParams(vmem_limit_bytes=16 << 20)

    def near(*values):
        return [pltpu.with_memory_space_constraint(x, pltpu.VMEM) for x in values]

    def far(*values):
        return [pltpu.with_memory_space_constraint(x, pltpu.HBM) for x in values]

    index = (jnp.arange(width, dtype=jnp.int32) % (width // 2)).astype(f32)
    freq = (ROPE_BASE ** (-(index * 2.0 / width)))[None, :]
    received = with_layout_constraint(to_sibling(key_value), Layout((0, 1, 2)))
    kv, q, *tables = pl.pallas_call(
        functools.partial(tables_kernel, half),
        out_shape=(
            local((rows, groups, pair), bf16),
            local((rows, heads, width), bf16),
            local((half * per, half), bf16),
            local((rows, width), f32),
            local((rows, width), f32),
            local((2, 4, 8, width), f32),
            local((2, 8, half), i32),
        ),
        in_specs=[vmem, hbm, hbm, hbm],
        out_specs=(vmem,) * 7,
        scratch_shapes=[pltpu.SMEM(doc_lengths.shape, i32), pltpu.SemaphoreType.DMA((3,))],
        cost_estimate=pl.CostEstimate(flops=10 ** 7, bytes_accessed=10 ** 6, transcendentals=10 ** 5),
        compiler_params=params,
        name="tables",
    )(*near(freq), *far(doc_lengths, key_value, queries))
    received, kv, q = lax.optimization_barrier((received, kv, q))
    core = lax.rem(lax.axis_index("ctx"), 2)
    first = core * half
    second = (1 - core) * half

    def take(x, start):
        return lax.dynamic_slice_in_dim(x, start, half, 0)

    own = jnp.concatenate([take(kv, first), take(received, first)], 0).transpose(1, 0, 2)
    own_other = jnp.concatenate([take(received, second), take(kv, second)], 0).transpose(1, 0, 2)

    own = pl.pallas_call(
        rotate_kernel,
        out_shape=local((groups, rows, pair), bf16),
        in_specs=[vmem] * 4,
        out_specs=vmem,
        cost_estimate=pl.CostEstimate(flops=10 ** 6, bytes_accessed=10 ** 6, transcendentals=0),
        compiler_params=params,
        name="rotate",
    )(*near(own, *tables[1:4]))

    one = along_chain(own, 1)
    two = along_chain(own, 2)

    state = (local((groups, half * per, 2 * width), f32), local((groups, half * per, width), f32))
    key_scratch = [pltpu.VMEM((2 * rows, half), bf16)]

    def begin(stream, own_keys):
        return pl.pallas_call(
            functools.partial(begin_kernel, half, factor, stream),
            out_shape=(local((groups, half * per, width), bf16),) + state,
            in_specs=[vmem] * 7,
            out_specs=(vmem,) * 3,
            scratch_shapes=[
                pltpu.VMEM((2, half, 1, width), f32),
                pltpu.VMEM((groups, rows, width), bf16),
                pltpu.VMEM((rows, half), bf16),
            ],
            cost_estimate=pl.CostEstimate(flops=10 ** 9, bytes_accessed=10 ** 6, transcendentals=10 ** 6),
            compiler_params=params,
        )(*near(q, *tables, own_keys))

    qrot0, acc0, top0 = begin(0, own)
    near_pair = jnp.stack([one, two])
    near_pair, acc0 = lax.optimization_barrier((near_pair, acc0))
    far_pair = along_chain(near_pair, 2)

    def middle(stream, qrot, acc, top, keys):
        return pl.pallas_call(
            functools.partial(middle_kernel, half, factor, stream),
            out_shape=state,
            in_specs=[vmem] * 9,
            out_specs=(vmem,) * 2,
            scratch_shapes=key_scratch,
            input_output_aliases={6: 0, 7: 1},
            cost_estimate=pl.CostEstimate(flops=10 ** 9, bytes_accessed=10 ** 6, transcendentals=10 ** 6),
            compiler_params=params,
        )(*near(qrot, *tables, acc, top, keys))

    acc0, top0 = middle(0, qrot0, acc0, top0, near_pair)
    near_pair, own_other, acc0 = lax.optimization_barrier((near_pair, own_other, acc0))
    near_other = to_sibling(near_pair)
    qrot1, acc1, top1 = begin(1, own_other)
    acc1, top1 = middle(1, qrot1, acc1, top1, near_other)

    far_pair, acc0, acc1 = lax.optimization_barrier((far_pair, acc0, acc1))
    far_keys = jnp.concatenate([far_pair[0], far_pair[1]], axis=1)
    far_other = to_sibling(jnp.concatenate([far_pair[0], far_pair[1, :, half:]], axis=1))

    def end(stream, qrot, acc, top, keys, *ready):
        sends = half * per // (2 * TILE) + 1
        result = (half, heads, width)
        return pl.pallas_call(
            functools.partial(end_kernel, half, factor, stream),
            out_shape=pltpu.HBM((rows, heads, width), bf16) if stream else local(result, bf16),
            in_specs=[vmem] * (9 + len(ready)),
            out_specs=hbm if stream else vmem,
            scratch_shapes=key_scratch + [pltpu.VMEM(result, bf16), pltpu.SemaphoreType.DMA((sends,))] * stream,
            cost_estimate=pl.CostEstimate(flops=10 ** 9, bytes_accessed=10 ** 6, transcendentals=10 ** 6),
            compiler_params=params,
        )(*near(qrot, *tables, acc, top, keys, *ready))

    first_half = end(0, qrot0, acc0, top0, far_keys)
    return end(1, qrot1, acc1, top1, far_other, first_half)


def solution(mesh):
    in_specs = (P("ctx", "tp", None), P("ctx", "tp", None), P())
    out_specs = P("ctx", "tp", None)
    return jax.shard_map(shards, mesh=mesh, in_specs=in_specs, out_specs=out_specs, check_vma=False)
```
